256 devices in a mesh: row: 32 (over z, y_hi, core), col: 8 (over y_lo, x).
Axes of the slice: x: 4, y: 4 (y_hi: 2, y_lo: 2; y = y_hi * 2 + y_lo), z: 8, core: 2. Of those that a mesh axis runs over, the one named last changes fastest.
Arguments:
- samples: float32 [512, 16384], P(None, 'col'), may hold values from -0.8 to 0.8
- values: float32 [16384, 16384], P('row', 'col'), may hold values from -6 to 6
- diag_entries: float32 [16384], P('row'), may hold values from 16 to 32
- block_mask: int32 [64, 64], replicated, may hold values 0 or 1
Outputs:
- updated: float32 [16384, 16384], P('row', 'col')
The draws below stay inside these ranges and needn't reach their ends.
All inputs are finite; a program needn't handle non-finite values.
Results may differ from the reference program's by a relative error of at most 0.0003.
Values sent between devices are 32-bit elements; how exact they have to be, the bound alone decides.
No kernel may reach another device: no remote copies, remote signals or barrier semaphores. Data moves between devices by JAX's collectives and lax.ppermute only.
A program may use at most 64 MiB of HBM per device.

```python
import math
import jax
import jax.numpy as jnp
from jax import lax

P_SIZE = 16384
BLOCKS = 64
SAMPLES = 512


def set_ends(entries, key, low, largest):
    longest = entries.shape.index(max(entries.shape))
    spots = []
    for shift in (0, 1):
        where = [jax.random.randint(jax.random.fold_in(key, axis), (), 0, length) for axis, length in enumerate(entries.shape)]
        where[longest] = (where[longest] + shift) % entries.shape[longest]
        spots.append(tuple(where))
    return entries.at[spots[0]].set(low).at[spots[1]].set(largest)


def spiked(result, key, source, target, parts, factor):
    owner, partner = [(jnp.arange(result.shape[dim]) // (result.shape[dim] // parts)).reshape([-1 if axis == dim else 1 for axis in range(result.ndim)]) for dim in (source, target)]
    chosen = jax.random.permutation(key, parts)[partner]
    strong = (owner == chosen) | (owner == (partner + parts // 2) % parts)
    return jnp.where(strong, factor * result, result)


def steps_of(stream_key, dims, shards, low, high):
    loudness, own = 1.0, jax.random.fold_in(stream_key, 6)
    for axis_at, shards_of in shards:
        heights = jnp.exp(jax.random.uniform(jax.random.fold_in(own, axis_at), (shards_of,), jnp.float32, low / len(shards), high / len(shards)))
        loudness = loudness * jnp.repeat(heights, dims[axis_at] // shards_of).reshape([-1 if axis == axis_at else 1 for axis in range(len(dims))])
    return loudness


def centred(key, extent, spread, most, cuts=(), held_as=jnp.bfloat16):
    values = jax.random.normal(key, extent, jnp.float32) * spread
    if len(cuts) > 0:
        values = steps_of(key, extent, cuts, -0.22, 0.18) * values
    return jnp.clip(values, min=-most, max=most).astype(held_as)


def noise_with(stream_key, shape, spread, reach, pieces, heavy, held_as=jnp.bfloat16):
    values = spread * jax.random.normal(stream_key, shape, jnp.float32)
    if pieces:
        values = values * steps_of(stream_key, shape, pieces, -0.22, 0.18)
    return jnp.clip(spiked(values, jax.random.fold_in(stream_key, 3), *heavy), -reach, reach).astype(held_as)


def setup_inputs(seed: int = 0) -> dict:
    keys = jax.random.split(jax.random.key(seed), 5)
    samples = noise_with(keys[0], (SAMPLES, P_SIZE), 0.13, 0.8, ((1, 8),), (1, 0, 8, 2.0), jnp.float32)
    values = centred(keys[1], (P_SIZE, P_SIZE), 1.0, 6.0, ((0, 32), (1, 8)), jnp.float32)
    diag_entries = jnp.clip(jnp.exp(math.log(32.0) - 0.6931472 * jax.random.uniform(keys[2], (P_SIZE,), jnp.float32) ** steps_of(keys[2], (P_SIZE,), ((0, 32),), -0.2, 0.2)), 16.0, 32.0)
    block_mask = set_ends((jax.random.randint(keys[3], (BLOCKS, BLOCKS), 0, 2) < 1).astype(jnp.int32), jax.random.fold_in(keys[3], 1), 0, 1)
    return dict(samples=samples, values=values, diag_entries=diag_entries, block_mask=block_mask)


step_size = 8.0
penalty = 0.05


def reference(samples, values, diag_entries, block_mask):
    order_total = values.shape[0]
    mask_block = order_total // BLOCKS
    dense_mask = jnp.repeat(jnp.repeat(block_mask, mask_block, axis=0), mask_block, axis=1).astype(jnp.float32)
    indices = jnp.arange(order_total, dtype=jnp.int32)
    on_diag = indices[:, None] == indices[None, :]
    omega = jnp.where(on_diag, diag_entries[:, None], dense_mask * values)
    projected = jnp.dot(samples, omega, precision=lax.Precision.HIGHEST, preferred_element_type=jnp.float32)
    sample_count = samples.shape[0]
    row_block = order_total // BLOCKS

    def update_rows(block_index):
        begin = (block_index * row_block).astype(jnp.int32)
        x_rows = lax.dynamic_slice_in_dim(samples, begin, row_block, 1)
        y_rows = lax.dynamic_slice_in_dim(projected, begin, row_block, 1)
        w_rows = lax.dot_general(x_rows, projected, (((0,), (0,)), ((), ())), precision=lax.Precision.HIGHEST, preferred_element_type=jnp.float32)
        wt_rows = lax.dot_general(y_rows, samples, (((0,), (0,)), ((), ())), precision=lax.Precision.HIGHEST, preferred_element_type=jnp.float32)
        gradient = 0.5 * (w_rows / sample_count + wt_rows / sample_count)
        row_ids = begin + jnp.arange(row_block, dtype=jnp.int32)
        diag_here = row_ids[:, None] == indices[None, :]
        diag_rows = lax.dynamic_slice_in_dim(diag_entries, begin, row_block, 0)
        gradient = gradient - jnp.where(diag_here, 1.0 / diag_rows[:, None], jnp.float32(0.0))
        omega_rows = lax.dynamic_slice_in_dim(omega, begin, row_block, 0)
        stepped = omega_rows - step_size * gradient
        shrunk = jnp.sign(stepped) * jnp.maximum(jnp.abs(stepped) - step_size * penalty, jnp.float32(0.0))
        return jnp.where(diag_here, stepped, shrunk)

    blocks_out = lax.map(update_rows, jnp.arange(BLOCKS, dtype=jnp.int32))
    return blocks_out.reshape(order_total, order_total)
```

```python
import itertools

import jax
import jax.numpy as jnp
from jax import lax
from jax.sharding import Mesh
from jax.sharding import PartitionSpec as P

ROW = ("z", "yh", "core")
COL = ("yl", "x")
ALL = ROW + COL
SIZES = (8, 2, 2, 2, 4)
Z = SIZES[0]

step_size = 8.0
penalty = 0.05


def moved(array, target):
    def place(z, yh, core, col):
        return ((z * 2 + yh) * 2 + core) * 8 + col

    everyone = itertools.product(range(8), range(2), range(2), range(8))
    return lax.ppermute(array, ALL, [(place(*at), place(*target(*at))) for at in everyone])


def swapped(array):
    return moved(array, lambda z, yh, core, col: (col, yh, core, z))


def up(array):
    return moved(array, lambda z, yh, core, col: ((z + 1) % Z, yh, core, col))


def down(array):
    return moved(array, lambda z, yh, core, col: ((z - 1) % Z, yh, core, col))


def both_ways(rising, falling):
    rising, falling = lax.optimization_barrier((rising, falling))
    return lax.optimization_barrier((up(rising), down(falling)))


def other_core(array):
    return moved(array, lambda z, yh, core, col: (z, yh, 1 - core, col))


def other_half(array):
    return moved(array, lambda z, yh, core, col: (z, 1 - yh, core, col))


def dot(left, right, contract):
    return lax.dot_general(
        left,
        right,
        (contract, ((), ())),
        precision=lax.Precision.HIGH,
        preferred_element_type=jnp.float32,
    )


def rows_of(array, index, count):
    return lax.dynamic_slice_in_dim(array, index * count, count, 0)


ORDER = (4, 3, -3, 2, -2, 1, -1, 0)


def per_device(samples, values, diag_entries, block_mask):
    tile_rows, tile_cols = values.shape
    sample_count = samples.shape[0]
    piece_rows = sample_count // Z
    half_rows = piece_rows // 2
    z, yh, core = (lax.axis_index(name) for name in ROW)
    col = lax.axis_index(COL)
    row_index = lax.axis_index(ROW)

    mine = lax.dynamic_slice(
        samples,
        (((col ^ 4) ^ z) * piece_rows, (yh * 2 + core) * tile_rows),
        (piece_rows, tile_rows),
    )
    first = swapped(mine)
    pieces = {4: first}
    for d in ORDER[1:]:
        pieces[d] = moved(
            first, lambda z, yh, core, col: (z, yh, core, (z ^ 4) ^ ((z + d) % Z) ^ col)
        )

    mask_block = samples.shape[1] * lax.axis_size(COL) // block_mask.shape[0]
    mask_rows = tile_rows // mask_block
    mask_cols = tile_cols // mask_block
    tile_mask = lax.dynamic_slice(
        block_mask, (row_index * mask_rows, col * mask_cols), (mask_rows, mask_cols)
    )
    mask_grid = tile_mask.astype(jnp.float32)[:, None, :, None]
    expanded = jnp.broadcast_to(mask_grid, (mask_rows, mask_block, mask_cols, mask_block)).reshape(
        tile_rows, tile_cols
    )
    row_ids = row_index * tile_rows + jnp.arange(tile_rows, dtype=jnp.int32)
    col_ids = col * tile_cols + jnp.arange(tile_cols, dtype=jnp.int32)
    on_diag = row_ids[:, None] == col_ids[None, :]
    omega = jnp.where(on_diag, diag_entries[:, None], expanded * values)

    own_x = jnp.concatenate([rows_of(pieces[d], core, half_rows) for d in ORDER])
    other_x = jnp.concatenate([rows_of(pieces[d], 1 - core, half_rows) for d in ORDER])
    other_part = dot(other_x, omega, ((1,), (0,)))
    own_part = dot(own_x, omega, ((1,), (0,)))
    both = own_part + other_core(other_part)
    part = {d: both[i * half_rows : (i + 1) * half_rows] for i, d in enumerate(ORDER)}
    cut = half_rows // 2
    rising, falling = both_ways(part[4][:cut], part[4][cut:])
    rising = part[3] + jnp.concatenate([rising, jnp.zeros_like(rising)])
    falling = part[-3] + jnp.concatenate([jnp.zeros_like(falling), falling])
    for d in (2, 1):
        rising, falling = both_ways(rising, falling)
        rising = part[d] + rising
        falling = part[-d] + falling
    rising, falling = both_ways(rising, falling)
    summed = part[0] + rising + falling
    summed = summed + other_half(summed)

    wanted = lax.dynamic_slice_in_dim(summed, yh * 2 * tile_rows, 2 * tile_rows, 1)
    arrived = swapped(wanted)
    kept = lax.dynamic_slice_in_dim(arrived, core * tile_rows, tile_rows, 1)
    given = other_core(lax.dynamic_slice_in_dim(arrived, (1 - core) * tile_rows, tile_rows, 1))
    zero = jnp.int32(0)
    piece = jnp.zeros((2, half_rows, tile_rows), jnp.float32)
    piece = lax.dynamic_update_slice(piece, kept[None], (core, zero, zero))
    piece = lax.dynamic_update_slice(piece, given[None], (1 - core, zero, zero))
    row_projected = jnp.zeros((Z, 2, half_rows, tile_rows), jnp.float32)
    for d in range(Z):
        if d:
            got = moved(piece, lambda z, yh, core, col: (z, yh, core, col ^ d))
        else:
            got = piece
        row_projected = lax.dynamic_update_slice(
            row_projected, got[None], (z ^ col ^ d, zero, zero, zero)
        )
    row_projected = row_projected.reshape(sample_count, tile_rows)

    whole = {0: summed}
    for d in (1, 2, 3):
        whole[-d] = up(whole[1 - d])
        whole[d] = down(whole[d - 1])
    whole[4] = jnp.concatenate([up(whole[-3][:cut]), down(whole[3][cut:])])
    own_y = jnp.concatenate([whole[d] for d in ORDER])
    other_y = other_core(own_y)

    mirrored = dot(row_projected, samples, ((0,), (0,)))
    product = dot(own_x, own_y, ((0,), (0,))) + dot(other_x, other_y, ((0,), (0,)))
    gradient = (product + mirrored) * (0.5 / sample_count) - jnp.where(
        on_diag, 1.0 / diag_entries[:, None], jnp.float32(0.0)
    )
    stepped = omega - step_size * gradient
    shrunk = jnp.sign(stepped) * jnp.maximum(
        jnp.abs(stepped) - step_size * penalty, jnp.float32(0.0)
    )
    return jnp.where(on_diag, stepped, shrunk)


def solution(mesh):
    split = Mesh(mesh.devices.reshape(SIZES), ALL)
    return jax.shard_map(
        per_device,
        mesh=split,
        in_specs=(P(None, COL), P(ROW, COL), P(ROW), P()),
        out_specs=P(ROW, COL),
        check_vma=False,
    )
```

```python
import functools
import itertools

import jax
import jax.numpy as jnp
from jax import lax
from jax.experimental import pallas as pl
from jax.experimental.pallas import tpu as pltpu
from jax.sharding import Mesh
from jax.sharding import PartitionSpec as P

ROW = ("z", "yh", "core")
COL = ("yl", "x")
ALL = ROW + COL
SIZES = (8, 2, 2, 2, 4)
Z = SIZES[0]

step_size = 8.0
penalty = 0.05


def moved(array, target):
    def place(z, yh, core, col):
        return ((z * 2 + yh) * 2 + core) * 8 + col

    everyone = itertools.product(range(8), range(2), range(2), range(8))
    return lax.ppermute(array, ALL, [(place(*at), place(*target(*at))) for at in everyone])


def swapped(array):
    return moved(array, lambda z, yh, core, col: (col, yh, core, z ^ col))


def up(array):
    return moved(array, lambda z, yh, core, col: ((z + 1) % Z, yh, core, col))


def down(array):
    return moved(array, lambda z, yh, core, col: ((z - 1) % Z, yh, core, col))


def both_ways(rising, falling):
    rising, falling = together(rising, falling)
    return together(up(rising), down(falling))


def together(*arrays):
    return lax.optimization_barrier(arrays)


def other_core(array):
    return moved(array, lambda z, yh, core, col: (z, yh, 1 - core, col))


def other_half(array):
    return moved(array, lambda z, yh, core, col: (z, 1 - yh, core, col))


def dot(left, right, contract):
    return lax.dot_general(
        left,
        right,
        (contract, ((), ())),
        precision=lax.Precision.HIGH,
        preferred_element_type=jnp.float32,
    )


LANES = 256


def split_in_two(array):
    high = array.astype(jnp.bfloat16)
    return high, (array - high.astype(jnp.float32)).astype(jnp.bfloat16)


def product_tile(step, left, right, high, low):
    @pl.when(step == 0)
    def _():
        high[...], low[...] = split_in_two(left[...].T)

    right_high, right_low = split_in_two(right[...])
    made = jnp.dot(low[...], right_high, preferred_element_type=jnp.float32)
    made += jnp.dot(high[...], right_low, preferred_element_type=jnp.float32)
    return made + jnp.dot(high[...], right_high, preferred_element_type=jnp.float32)


def product_kernel(left, right, out, high, low):
    out[...] = product_tile(pl.program_id(0), left, right, high, low)


def update_kernel(scale, offset, left, right, addend, omega, diag, out, high, low):
    step = pl.program_id(0)
    made = product_tile(step, left, right, high, low) + addend[...]
    behind = offset[0] - step * LANES
    rows = lax.broadcasted_iota(jnp.int32, made.shape, 0)
    cols = lax.broadcasted_iota(jnp.int32, made.shape, 1)
    on_diag = cols - rows == behind
    gradient = made * scale - jnp.where(on_diag, 1.0 / diag[...], jnp.float32(0.0))
    stepped = omega[...] - step_size * gradient
    limit = step_size * penalty
    out[...] = jnp.where(on_diag, stepped, stepped - jnp.clip(stepped, -limit, limit))


def product(left, right):
    depth, rows = left.shape
    cols = right.shape[1]
    whole = pl.BlockSpec((depth, rows), lambda j: (0, 0))
    return pl.pallas_call(
        product_kernel,
        grid=(cols // LANES,),
        in_specs=[whole, pl.BlockSpec((depth, LANES), lambda j: (0, j))],
        out_specs=pl.BlockSpec((rows, LANES), lambda j: (0, j)),
        out_shape=jax.ShapeDtypeStruct((rows, cols), jnp.float32),
        scratch_shapes=[pltpu.VMEM((rows, depth), jnp.bfloat16)] * 2,
        cost_estimate=pl.CostEstimate(
            flops=6 * depth * rows * cols,
            bytes_accessed=4 * (depth * rows + depth * cols + rows * cols),
            transcendentals=0,
        ),
        compiler_params=pltpu.CompilerParams(vmem_limit_bytes=16 << 20),
        name="product",
    )(left, right)


def updated_tile(scale, offset, left, right, addend, omega, diag):
    depth, rows = left.shape
    cols = right.shape[1]
    whole = pl.BlockSpec((depth, rows), lambda j, *_: (0, 0))
    tile = pl.BlockSpec((rows, LANES), lambda j, *_: (0, j))
    return pl.pallas_call(
        functools.partial(update_kernel, scale),
        grid_spec=pltpu.PrefetchScalarGridSpec(
            num_scalar_prefetch=1,
            grid=(cols // LANES,),
            in_specs=[
                whole,
                pl.BlockSpec((depth, LANES), lambda j, *_: (0, j)),
                tile,
                tile,
                pl.BlockSpec((rows, 1), lambda j, *_: (0, 0)),
            ],
            out_specs=tile,
            scratch_shapes=[pltpu.VMEM((rows, depth), jnp.bfloat16)] * 2,
        ),
        out_shape=jax.ShapeDtypeStruct((rows, cols), jnp.float32),
        cost_estimate=pl.CostEstimate(
            flops=6 * depth * rows * cols,
            bytes_accessed=4 * (depth * rows + depth * cols + 3 * rows * cols),
            transcendentals=0,
        ),
        compiler_params=pltpu.CompilerParams(vmem_limit_bytes=16 << 20),
        name="update",
    )(offset, left, right, addend, omega, diag)


def rows_of(array, index, count):
    return lax.dynamic_slice_in_dim(array, index * count, count, 0)


EARLY = (4, 3, -3)
LATE = (2, -2, 1, -1, 0)
NEAR = (0, 1, -1, 2)
FAR = (-2, 3, -3, 4)


def per_device(samples, values, diag_entries, block_mask):
    tile_rows, tile_cols = values.shape
    sample_count = samples.shape[0]
    piece_rows = sample_count // Z
    half_rows = piece_rows // 2
    cut = half_rows // 2
    z, yh, core = (lax.axis_index(name) for name in ROW)
    col = lax.axis_index(COL)
    row_index = lax.axis_index(ROW)

    mine = lax.dynamic_slice(
        samples,
        ((z ^ 4) * piece_rows, (yh * 2 + core) * tile_rows),
        (piece_rows, tile_rows),
    )
    first = swapped(mine)

    def piece_of(d):
        return moved(
            first, lambda z, yh, core, col: (z, yh, core, (z ^ 4) ^ ((z + d) % Z) ^ col)
        )

    pieces = {4: first}
    pieces[3], pieces[-3], first = together(piece_of(3), piece_of(-3), first)
    for d in LATE:
        pieces[d] = piece_of(d)

    mask_block = samples.shape[1] * lax.axis_size(COL) // block_mask.shape[0]
    mask_rows = tile_rows // mask_block
    mask_cols = tile_cols // mask_block
    tile_mask = lax.dynamic_slice(
        block_mask, (row_index * mask_rows, col * mask_cols), (mask_rows, mask_cols)
    )
    mask_lines = jnp.repeat(tile_mask.astype(jnp.float32), mask_block, axis=1)
    expanded = jnp.broadcast_to(
        mask_lines[:, None, :], (mask_rows, mask_block, tile_cols)
    ).reshape(tile_rows, tile_cols)
    row_ids = row_index * tile_rows + jnp.arange(tile_rows, dtype=jnp.int32)
    col_ids = col * tile_cols + jnp.arange(tile_cols, dtype=jnp.int32)
    on_diag = row_ids[:, None] == col_ids[None, :]
    omega = jnp.where(on_diag, diag_entries[:, None], expanded * values)

    own_x = {d: rows_of(pieces[d], core, half_rows) for d in pieces}
    other_x = {d: rows_of(pieces[d], 1 - core, half_rows) for d in pieces}

    def parts_of(order, sources):
        made = dot(jnp.concatenate([sources[d] for d in order]), omega, ((1,), (0,)))
        made = made.reshape(len(order), 2, half_rows, tile_cols)
        own = lax.dynamic_slice_in_dim(made, core, 1, 1)
        other = lax.dynamic_slice_in_dim(made, 1 - core, 1, 1)
        both = own + other_core(other)
        return {d: both[i, 0] for i, d in enumerate(order)}

    part = parts_of(EARLY, pieces)
    rising, falling = both_ways(part[4][:cut], part[4][cut:])
    rising, falling, *late = together(rising, falling, *(pieces[d] for d in LATE))
    part.update(parts_of(LATE, dict(zip(LATE, late, strict=True))))
    rising = part[3] + jnp.concatenate([rising, jnp.zeros_like(rising)])
    falling = part[-3] + jnp.concatenate([jnp.zeros_like(falling), falling])
    for d in (2, 1):
        rising, falling = both_ways(rising, falling)
        rising = part[d] + rising
        falling = part[-d] + falling
    rising, falling = both_ways(rising, falling)
    summed = part[0] + rising + falling
    summed = summed + other_half(summed)

    whole = {0: summed}
    wanted = lax.dynamic_slice_in_dim(summed, yh * 2 * tile_rows, 2 * tile_rows, 1)
    rising, falling, wanted = together(summed, summed, wanted)
    whole[-1], whole[1], arrived = together(up(rising), down(falling), swapped(wanted))

    kept = lax.dynamic_slice_in_dim(arrived, core * tile_rows, tile_rows, 1)
    given = lax.dynamic_slice_in_dim(arrived, (1 - core) * tile_rows, tile_rows, 1)
    rising, falling, given = together(whole[-1], whole[1], given)
    given = other_core(given)
    whole[-2] = up(rising)
    whole[2] = down(falling)
    zero = jnp.int32(0)
    piece = jnp.zeros((2, half_rows, tile_rows), jnp.float32)
    piece = lax.dynamic_update_slice(piece, kept[None], (core, zero, zero))
    piece = lax.dynamic_update_slice(piece, given[None], (1 - core, zero, zero))

    def got_of(d):
        return moved(piece, lambda z, yh, core, col: (z, yh, core, col ^ d))

    got = {0: piece, 1: got_of(1), 2: got_of(2), 4: got_of(4)}
    whole[-2], whole[2], got[1], got[2], got[4], piece = together(
        whole[-2], whole[2], got[1], got[2], got[4], piece
    )
    whole[-3] = up(whole[-2])
    whole[3] = down(whole[2])
    near_y = jnp.concatenate([whole[d] for d in NEAR])
    other_near_y = other_core(near_y)
    got.update({d: got_of(d) for d in (3, 5, 6, 7)})
    whole[-3], whole[3], *rest = together(
        whole[-3], whole[3], other_near_y, *(got[d] for d in (3, 5, 6, 7))
    )
    other_near_y = rest[0]
    got.update(zip((3, 5, 6, 7), rest[1:], strict=True))
    whole[4] = jnp.concatenate([up(whole[-3][:cut]), down(whole[3][cut:])])
    row_projected = jnp.zeros((Z, 2, half_rows, tile_rows), jnp.float32)
    for d in range(Z):
        row_projected = lax.dynamic_update_slice(
            row_projected, got[d][None], (col ^ d, zero, zero, zero)
        )
    row_projected = row_projected.reshape(sample_count, tile_rows)

    products = product(row_projected, samples)
    far_y = jnp.concatenate([whole[d] for d in FAR])
    far_y, products = together(far_y, products)
    other_far_y = other_core(far_y)

    order = (NEAR, FAR)
    all_x = jnp.concatenate([half[d] for some in order for half in (own_x, other_x) for d in some])
    all_y = jnp.concatenate([near_y, other_near_y, far_y, other_far_y])
    offset = (row_index * tile_rows - col * tile_cols).reshape(1)
    return updated_tile(
        0.5 / sample_count, offset, all_x, all_y, products, omega, diag_entries[:, None]
    )


def solution(mesh):
    split = Mesh(mesh.devices.reshape(SIZES), ALL)

    return jax.shard_map(
        per_device,
        mesh=split,
        in_specs=(P(None, COL), P(ROW, COL), P(ROW), P()),
        out_specs=P(ROW, COL),
        check_vma=False,
    )
```

```python
import functools
import itertools

import jax
import jax.numpy as jnp
from jax import lax
from jax.experimental import pallas as pl
from jax.experimental.pallas import tpu as pltpu
from jax.sharding import Mesh
from jax.sharding import PartitionSpec as P

ROW = ("z", "yh", "core")
COL = ("yl", "x")
ALL = ROW + COL
SIZES = (8, 2, 2, 2, 4)
Z = SIZES[0]

step_size = 8.0
penalty = 0.05


def moved(array, target):
    def place(z, yh, core, col):
        return ((z * 2 + yh) * 2 + core) * 8 + col

    everyone = itertools.product(range(8), range(2), range(2), range(8))
    return lax.ppermute(array, ALL, [(place(*at), place(*target(*at))) for at in everyone])


def swapped(array):
    return moved(array, lambda z, yh, core, col: (col, yh, core, z ^ col))


def up(array):
    return moved(array, lambda z, yh, core, col: ((z + 1) % Z, yh, core, col))


def down(array):
    return moved(array, lambda z, yh, core, col: ((z - 1) % Z, yh, core, col))


def both_ways(rising, falling):
    rising, falling = together(rising, falling)
    return together(up(rising), down(falling))


def together(*arrays):
    return lax.optimization_barrier(arrays)


def other_core(array):
    return moved(array, lambda z, yh, core, col: (z, yh, 1 - core, col))


def other_half(array):
    return moved(array, lambda z, yh, core, col: (z, 1 - yh, core, col))


LANES = 512


def in_hbm(array):
    return pltpu.with_memory_space_constraint(array, pltpu.HBM)


def split_in_two(array):
    high = array.astype(jnp.bfloat16)
    return high, (array - high.astype(jnp.float32)).astype(jnp.bfloat16)


def in_three(left, right):
    made = jnp.dot(left[1], right[0], preferred_element_type=jnp.float32)
    made += jnp.dot(left[0], right[1], preferred_element_type=jnp.float32)
    return made + jnp.dot(left[0], right[0], preferred_element_type=jnp.float32)


def dot(left, right):
    return jnp.dot(
        left, right, precision=lax.Precision.HIGH, preferred_element_type=jnp.float32
    )


def product_kernel(scale, sizes, at, *refs):
    xs, refs = refs[: sizes[0]], refs[sizes[0] :]
    others, refs = refs[: sizes[1]], refs[sizes[1] :]
    ys, samples, refs = refs[:2], refs[2], refs[3:]
    *final, out, high, low = refs
    step = pl.program_id(0)
    piece_rows = xs[0].shape[0]
    half = piece_rows // 2

    @pl.when(step == 0)
    def _():
        rows = []
        for which in (at[1], 1 - at[1]):
            rows += [x[pl.ds(pl.multiple_of(which * half, half), half), :] for x in xs]
        rows += [other[...] for other in others]
        high[...], low[...] = split_in_two(jnp.concatenate(rows).T)

    right = [y[...] for y in ys]
    for i in range(high.shape[1] // piece_rows - len(xs)):
        first = pl.multiple_of(at[2 + i] * piece_rows, piece_rows)
        right.append(samples[pl.ds(first, piece_rows), :])
    made = in_three((high[...], low[...]), split_in_two(jnp.concatenate(right)))
    if scale is None:
        out[...] = made
        return
    addend, omega, diag = final
    made = made + addend[...]
    behind = at[0] - step * LANES
    rows = lax.broadcasted_iota(jnp.int32, made.shape, 0)
    cols = lax.broadcasted_iota(jnp.int32, made.shape, 1)
    on_diag = cols - rows == behind
    gradient = made * scale - jnp.where(on_diag, 1.0 / diag[...], jnp.float32(0.0))
    stepped = omega[...] - step_size * gradient
    limit = step_size * penalty
    out[...] = jnp.where(on_diag, stepped, stepped - jnp.clip(stepped, -limit, limit))


def product(at, xs, others, ys, samples, scale=None, final=()):
    depth = sum(part.shape[0] for part in (*xs, *others))
    rows, cols = xs[0].shape[1], samples.shape[1]

    def whole(array):
        return pl.BlockSpec(array.shape, lambda j, *_: (0, 0))

    def tile(array):
        return pl.BlockSpec((array.shape[0], LANES), lambda j, *_: (0, j))

    xs, samples = [in_hbm(x) for x in xs], in_hbm(samples)
    if final:
        final = [in_hbm(final[0]), in_hbm(final[1]), final[2]]
    specs = [whole(part) for part in (*xs, *others)] + [tile(part) for part in (*ys, samples)]
    specs += [whole(part) if part.shape[1] == 1 else tile(part) for part in final]
    return pl.pallas_call(
        functools.partial(product_kernel, scale, (len(xs), len(others))),
        grid_spec=pltpu.PrefetchScalarGridSpec(
            num_scalar_prefetch=1,
            grid=(cols // LANES,),
            in_specs=specs,
            out_specs=pl.BlockSpec((rows, LANES), lambda j, *_: (0, j)),
            scratch_shapes=[pltpu.VMEM((rows, depth), jnp.bfloat16)] * 2,
        ),
        out_shape=pltpu.HBM((rows, cols), jnp.float32),
        cost_estimate=pl.CostEstimate(
            flops=6 * depth * rows * cols,
            bytes_accessed=4 * (depth * rows + depth * cols + (1 + len(final)) * rows * cols),
            transcendentals=0,
        ),
        compiler_params=pltpu.CompilerParams(vmem_limit_bytes=16 << 20),
        name="product",
    )(at, *xs, *others, *ys, samples, *final)


NEXT = (3, -3)
LATE = (2, -2, 1, -1, 0)
NEAR = (0, 1, -1, 2)
FAR = (-2, 3, -3, 4)


def per_device(samples, values, diag_entries, block_mask):
    tile_rows, tile_cols = values.shape
    sample_count = samples.shape[0]
    piece_rows = sample_count // Z
    half_rows = piece_rows // 2
    cut = half_rows // 2
    z, yh, core = (lax.axis_index(name) for name in ROW)
    col = lax.axis_index(COL)
    row_index = lax.axis_index(ROW)

    mine = lax.dynamic_slice(
        samples,
        ((z ^ 4) * piece_rows, (yh * 2 + core) * tile_rows),
        (piece_rows, tile_rows),
    )
    first = swapped(mine)

    def piece_of(d):
        return moved(
            first, lambda z, yh, core, col: (z, yh, core, (z ^ 4) ^ ((z + d) % Z) ^ col)
        )

    pieces = {4: first}
    pieces[3], pieces[-3], first = together(piece_of(3), piece_of(-3), first)
    pieces.update({d: piece_of(d) for d in LATE})

    mask_block = samples.shape[1] * lax.axis_size(COL) // block_mask.shape[0]
    mask_rows = tile_rows // mask_block
    mask_cols = tile_cols // mask_block
    tile_mask = lax.dynamic_slice(
        block_mask, (row_index * mask_rows, col * mask_cols), (mask_rows, mask_cols)
    )
    mask_lines = jnp.repeat(tile_mask.astype(jnp.float32), mask_block, axis=1)
    expanded = jnp.broadcast_to(
        mask_lines[:, None, :], (mask_rows, mask_block, tile_cols)
    ).reshape(tile_rows, tile_cols)
    row_ids = row_index * tile_rows + jnp.arange(tile_rows, dtype=jnp.int32)
    col_ids = col * tile_cols + jnp.arange(tile_cols, dtype=jnp.int32)
    on_diag = row_ids[:, None] == col_ids[None, :]
    omega = jnp.where(on_diag, diag_entries[:, None], expanded * values)

    def parts_of(order, sources):
        made = dot(jnp.concatenate([sources[d] for d in order]), omega)
        made = made.reshape(len(order), 2, half_rows, tile_cols)
        own = lax.dynamic_slice_in_dim(made, core, 1, 1)
        other = lax.dynamic_slice_in_dim(made, 1 - core, 1, 1)
        both = own + other_core(other)
        return {d: both[i, 0] for i, d in enumerate(order)}

    part = parts_of((4,), pieces)
    rising, falling = both_ways(part[4][:cut], part[4][cut:])
    part.update(parts_of(NEXT, pieces))
    rising = part[3] + jnp.concatenate([rising, jnp.zeros_like(rising)])
    falling = part[-3] + jnp.concatenate([jnp.zeros_like(falling), falling])
    rising, falling = both_ways(rising, falling)
    part.update(parts_of(LATE, pieces))
    rising, falling = both_ways(part[2] + rising, part[-2] + falling)
    rising, falling = part[1] + rising, part[-1] + falling
    rising, falling = both_ways(rising, falling)
    summed = part[0] + rising + falling
    summed = summed + other_half(summed)

    whole = {0: summed}
    wanted = lax.dynamic_slice_in_dim(summed, yh * 2 * tile_rows, 2 * tile_rows, 1)
    rising, falling, wanted = together(summed, summed, wanted)
    whole[-1], whole[1] = together(up(rising), down(falling))
    arrived = swapped(wanted)
    whole[-2], whole[2] = together(up(whole[-1]), down(whole[1]))
    kept = lax.dynamic_slice_in_dim(arrived, core * tile_rows, tile_rows, 1)
    given = lax.dynamic_slice_in_dim(arrived, (1 - core) * tile_rows, tile_rows, 1)
    given = other_core(given)
    zero = jnp.int32(0)
    piece = jnp.zeros((2, half_rows, tile_rows), jnp.float32)
    piece = lax.dynamic_update_slice(piece, kept[None], (core, zero, zero))
    piece = lax.dynamic_update_slice(piece, given[None], (1 - core, zero, zero))
    piece = piece.reshape(piece_rows, tile_rows)
    facing = moved(piece, lambda z, yh, core, col: (z, yh, core, col ^ 4))
    near_y = jnp.concatenate([whole[d] for d in NEAR])
    pair = jnp.concatenate([piece, facing])

    def along_x(array, by):
        return moved(
            array, lambda z, yh, core, col: (z, yh, core, col // 4 * 4 + (col % 4 + by) % 4)
        )

    whole[-3], whole[3] = together(up(whole[-2]), down(whole[2]))
    before, after = along_x(pair, 1), along_x(pair, -1)
    other_near_y = other_core(near_y)
    offset = row_index * tile_rows - col * tile_cols
    x_at, side = col % 4, col // 4
    match = [
        flip * 4 + (x_at + by) % 4 for by in (0, -1, 1, 2) for flip in (side, 1 - side)
    ]
    rising, falling = up(whole[-3][:cut]), down(whole[3][cut:])
    before, after, pair = together(before, after, pair)
    opposite = along_x(pair, 2)
    products = product(
        jnp.stack([offset, core, *match[:4]]),
        [pieces[d] for d in NEAR],
        [pair, before],
        [near_y, other_near_y],
        samples,
    )
    far_y = jnp.concatenate([whole[d] for d in FAR[:-1]] + [rising, falling])
    other_far_y = other_core(far_y)
    return product(
        jnp.stack([offset, core, *match[4:]]),
        [pieces[d] for d in FAR],
        [after, opposite],
        [far_y, other_far_y],
        samples,
        0.5 / sample_count,
        [products, omega, diag_entries[:, None]],
    )


def solution(mesh):
    split = Mesh(mesh.devices.reshape(SIZES), ALL)

    return jax.shard_map(
        per_device,
        mesh=split,
        in_specs=(P(None, COL), P(ROW, COL), P(ROW), P()),
        out_specs=P(ROW, COL),
        check_vma=False,
    )
```

```python
import functools
import itertools

import jax
import jax.numpy as jnp
from jax import lax
from jax.experimental import pallas as pl
from jax.experimental.pallas import tpu as pltpu
from jax.sharding import Mesh
from jax.sharding import PartitionSpec as P

ROW = ("z", "yh", "core")
COL = ("yl", "x")
ALL = ROW + COL
SIZES = (8, 2, 2, 2, 4)
Z = SIZES[0]

step_size = 8.0
penalty = 0.05


def moved(array, target):
    def place(z, yh, core, col):
        return ((z * 2 + yh) * 2 + core) * 8 + col

    everyone = itertools.product(range(8), range(2), range(2), range(8))
    return lax.ppermute(array, ALL, [(place(*at), place(*target(*at))) for at in everyone])


def swapped(array):
    return moved(array, lambda z, yh, core, col: (col, yh, core, z ^ col))


def up(array):
    return moved(array, lambda z, yh, core, col: ((z + 1) % Z, yh, core, col))


def down(array):
    return moved(array, lambda z, yh, core, col: ((z - 1) % Z, yh, core, col))


def both_ways(rising, falling):
    rising, falling = together(rising, falling)
    return together(up(rising), down(falling))


def together(*arrays):
    return lax.optimization_barrier(arrays)


def other_core(array):
    return moved(array, lambda z, yh, core, col: (z, yh, 1 - core, col))


def other_half(array):
    return moved(array, lambda z, yh, core, col: (z, 1 - yh, core, col))


LANES = 512


def in_hbm(array):
    return pltpu.with_memory_space_constraint(array, pltpu.HBM)


def split_in_two(array):
    high = array.astype(jnp.bfloat16)
    return high, (array - high.astype(jnp.float32)).astype(jnp.bfloat16)


def in_three(left, right):
    made = jnp.dot(left[1], right[0], preferred_element_type=jnp.float32)
    made += jnp.dot(left[0], right[1], preferred_element_type=jnp.float32)
    return made + jnp.dot(left[0], right[0], preferred_element_type=jnp.float32)


def dot(left, right):
    return jnp.dot(
        left, right, precision=lax.Precision.HIGH, preferred_element_type=jnp.float32
    )


def columns_kernel(count, core, *refs):
    xs, rights, (out, high, low) = refs[:count], refs[count:-3], refs[-3:]

    @pl.when(pl.program_id(0) == 0)
    def _():
        half = xs[0].shape[0] // 2
        rows = []
        for some in (xs[: count // 2], xs[count // 2 :]):
            for which in (core[0], 1 - core[0]):
                rows += [x[pl.ds(pl.multiple_of(which * half, half), half), :] for x in some]
        high[...], low[...] = split_in_two(jnp.concatenate(rows).T)

    right = jnp.concatenate([part[...] for part in rights])
    out[...] = in_three((high[...], low[...]), split_in_two(right))


def update_kernel(scale, sizes, at, *refs):
    lefts, refs = refs[: sizes[0]], refs[sizes[0] :]
    rights, refs = refs[: sizes[1]], refs[sizes[1] :]
    addend, omega, diag, out, high, low = refs
    step = pl.program_id(0)

    @pl.when(step == 0)
    def _():
        high[...], low[...] = split_in_two(jnp.concatenate([part[...] for part in lefts]).T)

    right = jnp.concatenate([part[...] for part in rights])
    made = in_three((high[...], low[...]), split_in_two(right)) + addend[...]
    behind = at[0] - step * LANES
    rows = lax.broadcasted_iota(jnp.int32, made.shape, 0)
    cols = lax.broadcasted_iota(jnp.int32, made.shape, 1)
    on_diag = cols - rows == behind
    gradient = made * scale - jnp.where(on_diag, 1.0 / diag[...], jnp.float32(0.0))
    stepped = omega[...] - step_size * gradient
    limit = step_size * penalty
    out[...] = jnp.where(on_diag, stepped, stepped - jnp.clip(stepped, -limit, limit))


def whole(array):
    return pl.BlockSpec(array.shape, lambda j, *_: (0, 0))


def tile(array):
    return pl.BlockSpec((array.shape[0], LANES), lambda j, *_: (0, j))


def call(kernel, scalars, operands, specs, depth, rows, cols, out_shape):
    return pl.pallas_call(
        kernel,
        grid_spec=pltpu.PrefetchScalarGridSpec(
            num_scalar_prefetch=1,
            grid=(cols // LANES,),
            in_specs=specs,
            out_specs=pl.BlockSpec((rows, LANES), lambda j, *_: (0, j)),
            scratch_shapes=[pltpu.VMEM((rows, depth), jnp.bfloat16)] * 2,
        ),
        out_shape=out_shape,
        cost_estimate=pl.CostEstimate(
            flops=6 * depth * rows * cols,
            bytes_accessed=4 * (depth * rows + depth * cols + 2 * rows * cols),
            transcendentals=0,
        ),
        compiler_params=pltpu.CompilerParams(vmem_limit_bytes=16 << 20),
    )(scalars, *operands)


def columns_product(core, xs, rights):
    depth = sum(part.shape[0] for part in rights)
    rows, cols = xs[0].shape[1], rights[0].shape[1]
    xs = [in_hbm(x) for x in xs]
    return call(
        functools.partial(columns_kernel, len(xs)),
        core.reshape(1),
        [*xs, *rights],
        [whole(x) for x in xs] + [tile(part) for part in rights],
        depth,
        rows,
        cols,
        pltpu.HBM((rows, cols), jnp.float32),
    )


def updated(scale, offset, lefts, samples, order, addend, omega, diag):
    depth, cols = samples.shape
    rows = lefts[0].shape[1]
    samples, addend, omega = in_hbm(samples), in_hbm(addend), in_hbm(omega)
    piece_rows = depth // len(order)

    def piece(i):
        return pl.BlockSpec((piece_rows, LANES), lambda j, at: (at[1 + i], j))

    count = len(order)
    return call(
        functools.partial(update_kernel, scale, (len(lefts), count)),
        jnp.stack([offset, *order]),
        [*lefts, *[samples] * count, addend, omega, diag],
        [whole(part) for part in lefts]
        + [piece(i) for i in range(count)]
        + [tile(addend), tile(omega), whole(diag)],
        depth,
        rows,
        cols,
        jax.ShapeDtypeStruct((rows, cols), jnp.float32),
    )


NEXT = (3, -3)
LATE = (2, -2, 1, -1, 0)
NEAR = (0, 1, -1, 2)
FAR = (-2, 3, -3, 4)


def per_device(samples, values, diag_entries, block_mask):
    tile_rows, tile_cols = values.shape
    sample_count = samples.shape[0]
    piece_rows = sample_count // Z
    half_rows = piece_rows // 2
    cut = half_rows // 2
    z, yh, core = (lax.axis_index(name) for name in ROW)
    col = lax.axis_index(COL)
    row_index = lax.axis_index(ROW)

    mine = lax.dynamic_slice(
        samples,
        ((z ^ 4) * piece_rows, (yh * 2 + core) * tile_rows),
        (piece_rows, tile_rows),
    )
    first = swapped(mine)

    def piece_of(d):
        return moved(
            first, lambda z, yh, core, col: (z, yh, core, (z ^ 4) ^ ((z + d) % Z) ^ col)
        )

    pieces = {4: first}
    pieces[3], pieces[-3], first = together(piece_of(3), piece_of(-3), first)
    pieces.update({d: piece_of(d) for d in LATE})

    mask_block = samples.shape[1] * lax.axis_size(COL) // block_mask.shape[0]
    mask_rows = tile_rows // mask_block
    mask_cols = tile_cols // mask_block
    tile_mask = lax.dynamic_slice(
        block_mask, (row_index * mask_rows, col * mask_cols), (mask_rows, mask_cols)
    )
    mask_lines = jnp.repeat(tile_mask.astype(jnp.float32), mask_block, axis=1)
    expanded = jnp.broadcast_to(
        mask_lines[:, None, :], (mask_rows, mask_block, tile_cols)
    ).reshape(tile_rows, tile_cols)
    row_ids = row_index * tile_rows + jnp.arange(tile_rows, dtype=jnp.int32)
    col_ids = col * tile_cols + jnp.arange(tile_cols, dtype=jnp.int32)
    on_diag = row_ids[:, None] == col_ids[None, :]
    omega = jnp.where(on_diag, diag_entries[:, None], expanded * values)

    def parts_of(order, sources):
        made = dot(jnp.concatenate([sources[d] for d in order]), omega)
        made = made.reshape(len(order), 2, half_rows, tile_cols)
        own = lax.dynamic_slice_in_dim(made, core, 1, 1)
        other = lax.dynamic_slice_in_dim(made, 1 - core, 1, 1)
        both = own + other_core(other)
        return {d: both[i, 0] for i, d in enumerate(order)}

    part = parts_of((4,), pieces)
    rising, falling = both_ways(part[4][:cut], part[4][cut:])
    part.update(parts_of(NEXT, pieces))
    rising = part[3] + jnp.concatenate([rising, jnp.zeros_like(rising)])
    falling = part[-3] + jnp.concatenate([jnp.zeros_like(falling), falling])
    rising, falling = both_ways(rising, falling)
    part.update(parts_of(LATE, pieces))
    rising, falling = both_ways(part[2] + rising, part[-2] + falling)
    rising, falling = part[1] + rising, part[-1] + falling
    rising, falling = both_ways(rising, falling)
    summed = part[0] + rising + falling
    summed = summed + other_half(summed)

    whole = {0: summed}
    wanted = lax.dynamic_slice_in_dim(summed, yh * 2 * tile_rows, 2 * tile_rows, 1)
    rising, falling, wanted = together(summed, summed, wanted)
    whole[-1], whole[1] = together(up(rising), down(falling))
    arrived = swapped(wanted)
    whole[-2], whole[2] = together(up(whole[-1]), down(whole[1]))
    kept = lax.dynamic_slice_in_dim(arrived, core * tile_rows, tile_rows, 1)
    given = lax.dynamic_slice_in_dim(arrived, (1 - core) * tile_rows, tile_rows, 1)
    given = other_core(given)
    zero = jnp.int32(0)
    piece = jnp.zeros((2, half_rows, tile_rows), jnp.float32)
    piece = lax.dynamic_update_slice(piece, kept[None], (core, zero, zero))
    piece = lax.dynamic_update_slice(piece, given[None], (1 - core, zero, zero))
    piece = piece.reshape(piece_rows, tile_rows)
    facing = moved(piece, lambda z, yh, core, col: (z, yh, core, col ^ 4))
    near_y = jnp.concatenate([whole[d] for d in NEAR])
    pair = jnp.concatenate([piece, facing])

    def along_x(array, by):
        return moved(
            array, lambda z, yh, core, col: (z, yh, core, col // 4 * 4 + (col % 4 + by) % 4)
        )

    whole[-3], whole[3] = together(up(whole[-2]), down(whole[2]))
    before, after = along_x(pair, 1), along_x(pair, -1)
    other_near_y = other_core(near_y)
    opposite = along_x(pair, 2)
    rising, falling = together(up(whole[-3][:cut]), down(whole[3][cut:]))
    far_y = jnp.concatenate([whole[d] for d in FAR[:-1]] + [rising, falling])
    other_far_y = other_core(far_y)
    products = columns_product(
        core, [pieces[d] for d in NEAR + FAR], [near_y, other_near_y, far_y, other_far_y]
    )

    x_at, side = col % 4, col // 4
    match = [
        flip * 4 + (x_at + by) % 4 for by in (0, -1, 1, 2) for flip in (side, 1 - side)
    ]
    return updated(
        0.5 / sample_count,
        row_index * tile_rows - col * tile_cols,
        [pair, before, after, opposite],
        samples,
        match,
        products,
        omega,
        diag_entries[:, None],
    )


def solution(mesh):
    split = Mesh(mesh.devices.reshape(SIZES), ALL)

    return jax.shard_map(
        per_device,
        mesh=split,
        in_specs=(P(None, COL), P(ROW, COL), P(ROW), P()),
        out_specs=P(ROW, COL),
        check_vma=False,
    )
```

```python
import functools
import itertools

import jax
import jax.numpy as jnp
from jax import lax
from jax.experimental import pallas as pl
from jax.experimental.pallas import tpu as pltpu
from jax.sharding import Mesh
from jax.sharding import PartitionSpec as P

ROW = ("z", "yh", "core")
COL = ("yl", "x")
ALL = ROW + COL
SIZES = (8, 2, 2, 2, 4)
Z = SIZES[0]

step_size = 8.0
penalty = 0.05


def moved(array, target):
    def place(z, yh, core, col):
        return ((z * 2 + yh) * 2 + core) * 8 + col

    everyone = itertools.product(range(8), range(2), range(2), range(8))
    return lax.ppermute(array, ALL, [(place(*at), place(*target(*at))) for at in everyone])


def swapped(array):
    return moved(array, lambda z, yh, core, col: (col, yh, core, z ^ col))


def up(array):
    return moved(array, lambda z, yh, core, col: ((z + 1) % Z, yh, core, col))


def down(array):
    return moved(array, lambda z, yh, core, col: ((z - 1) % Z, yh, core, col))


def both_ways(rising, falling):
    rising, falling = together(rising, falling)
    return together(up(rising), down(falling))


def together(*arrays):
    return lax.optimization_barrier(arrays)


def other_core(array):
    return moved(array, lambda z, yh, core, col: (z, yh, 1 - core, col))


def other_half(array):
    return moved(array, lambda z, yh, core, col: (z, 1 - yh, core, col))


LANES = 256


def in_hbm(array):
    return pltpu.with_memory_space_constraint(array, pltpu.HBM)


def split_in_two(array):
    high = array.astype(jnp.bfloat16)
    return high, (array - high.astype(jnp.float32)).astype(jnp.bfloat16)


def in_three(left, right):
    made = jnp.dot(left[1], right[0], preferred_element_type=jnp.float32)
    made += jnp.dot(left[0], right[1], preferred_element_type=jnp.float32)
    return made + jnp.dot(left[0], right[0], preferred_element_type=jnp.float32)


def dot(left, right):
    return jnp.dot(
        left, right, precision=lax.Precision.HIGH, preferred_element_type=jnp.float32
    )


def columns_kernel(count, core, *refs):
    xs, rights, (out, high, low) = refs[:count], refs[count:-3], refs[-3:]

    @pl.when(pl.program_id(0) == 0)
    def _():
        half = xs[0].shape[0] // 2
        rows = []
        for some in (xs[: count // 2], xs[count // 2 :]):
            for which in (core[0], 1 - core[0]):
                rows += [x[pl.ds(pl.multiple_of(which * half, half), half), :] for x in some]
        high[...], low[...] = split_in_two(jnp.concatenate(rows).T)

    right = jnp.concatenate([part[...] for part in rights])
    out[...] = in_three((high[...], low[...]), split_in_two(right))


def update_kernel(scale, sizes, at, *refs):
    lefts, refs = refs[: sizes[0]], refs[sizes[0] :]
    rights, refs = refs[: sizes[1]], refs[sizes[1] :]
    addend, omega, diag, out, high, low = refs
    step = pl.program_id(0)

    @pl.when(step == 0)
    def _():
        high[...], low[...] = split_in_two(jnp.concatenate([part[...] for part in lefts]).T)

    right = jnp.concatenate([part[...] for part in rights])
    made = in_three((high[...], low[...]), split_in_two(right)) + addend[...]
    behind = at[0] - step * LANES
    rows = lax.broadcasted_iota(jnp.int32, made.shape, 0)
    cols = lax.broadcasted_iota(jnp.int32, made.shape, 1)
    on_diag = cols - rows == behind
    gradient = made * scale - jnp.where(on_diag, 1.0 / diag[...], jnp.float32(0.0))
    stepped = omega[...] - step_size * gradient
    limit = step_size * penalty
    out[...] = jnp.where(on_diag, stepped, stepped - jnp.clip(stepped, -limit, limit))


def whole(array):
    return pl.BlockSpec(array.shape, lambda j, *_: (0, 0))


def tile(array):
    return pl.BlockSpec((array.shape[0], LANES), lambda j, *_: (0, j))


def call(kernel, scalars, operands, specs, depth, rows, cols, out_shape):
    return pl.pallas_call(
        kernel,
        grid_spec=pltpu.PrefetchScalarGridSpec(
            num_scalar_prefetch=1,
            grid=(cols // LANES,),
            in_specs=specs,
            out_specs=pl.BlockSpec((rows, LANES), lambda j, *_: (0, j)),
            scratch_shapes=[pltpu.VMEM((rows, depth), jnp.bfloat16)] * 2,
        ),
        out_shape=out_shape,
        cost_estimate=pl.CostEstimate(
            flops=6 * depth * rows * cols,
            bytes_accessed=4 * (depth * rows + depth * cols + 2 * rows * cols),
            transcendentals=0,
        ),
        compiler_params=pltpu.CompilerParams(vmem_limit_bytes=16 << 20),
    )(scalars, *operands)


def columns_product(core, xs, rights):
    depth = sum(part.shape[0] for part in rights)
    rows, cols = xs[0].shape[1], rights[0].shape[1]
    xs = [in_hbm(x) for x in xs]
    return call(
        functools.partial(columns_kernel, len(xs)),
        core.reshape(1),
        [*xs, *rights],
        [whole(x) for x in xs] + [tile(part) for part in rights],
        depth,
        rows,
        cols,
        jax.ShapeDtypeStruct((rows, cols), jnp.float32),
    )


def updated(scale, offset, lefts, samples, order, addend, omega, diag):
    depth, cols = samples.shape
    rows = lefts[0].shape[1]
    samples = in_hbm(samples)
    piece_rows = depth // len(order)

    def piece(i):
        return pl.BlockSpec((piece_rows, LANES), lambda j, at: (at[1 + i], j))

    count = len(order)
    return call(
        functools.partial(update_kernel, scale, (len(lefts), count)),
        jnp.stack([offset, *order]),
        [*lefts, *[samples] * count, addend, omega, diag],
        [whole(part) for part in lefts]
        + [piece(i) for i in range(count)]
        + [tile(addend), tile(omega), whole(diag)],
        depth,
        rows,
        cols,
        jax.ShapeDtypeStruct((rows, cols), jnp.float32),
    )


NEXT = (3, -3)
LATE = (2, -2, 1, -1, 0)
NEAR = (0, 1, -1, 2)
FAR = (-2, 3, -3, 4)


def per_device(samples, values, diag_entries, block_mask):
    tile_rows, tile_cols = values.shape
    sample_count = samples.shape[0]
    piece_rows = sample_count // Z
    half_rows = piece_rows // 2
    cut = half_rows // 2
    z, yh, core = (lax.axis_index(name) for name in ROW)
    col = lax.axis_index(COL)
    row_index = lax.axis_index(ROW)

    mine = lax.dynamic_slice(
        samples,
        ((z ^ 4) * piece_rows, (yh * 2 + core) * tile_rows),
        (piece_rows, tile_rows),
    )
    first = swapped(mine)

    def piece_of(d):
        return moved(
            first, lambda z, yh, core, col: (z, yh, core, (z ^ 4) ^ ((z + d) % Z) ^ col)
        )

    pieces = {4: first}
    pieces[3], pieces[-3], first = together(piece_of(3), piece_of(-3), first)
    pieces.update({d: piece_of(d) for d in LATE})

    mask_block = samples.shape[1] * lax.axis_size(COL) // block_mask.shape[0]
    mask_rows = tile_rows // mask_block
    mask_cols = tile_cols // mask_block
    tile_mask = lax.dynamic_slice(
        block_mask, (row_index * mask_rows, col * mask_cols), (mask_rows, mask_cols)
    )
    mask_lines = jnp.repeat(tile_mask.astype(jnp.float32), mask_block, axis=1)
    expanded = jnp.broadcast_to(
        mask_lines[:, None, :], (mask_rows, mask_block, tile_cols)
    ).reshape(tile_rows, tile_cols)
    row_ids = row_index * tile_rows + jnp.arange(tile_rows, dtype=jnp.int32)
    col_ids = col * tile_cols + jnp.arange(tile_cols, dtype=jnp.int32)
    on_diag = row_ids[:, None] == col_ids[None, :]
    omega = jnp.where(on_diag, diag_entries[:, None], expanded * values)

    def parts_of(order, sources):
        made = dot(jnp.concatenate([sources[d] for d in order]), omega)
        made = made.reshape(len(order), 2, half_rows, tile_cols)
        own = lax.dynamic_slice_in_dim(made, core, 1, 1)
        other = lax.dynamic_slice_in_dim(made, 1 - core, 1, 1)
        both = own + other_core(other)
        return {d: both[i, 0] for i, d in enumerate(order)}

    part = parts_of((4,), pieces)
    rising, falling = both_ways(part[4][:cut], part[4][cut:])
    part.update(parts_of(NEXT, pieces))
    rising = part[3] + jnp.concatenate([rising, jnp.zeros_like(rising)])
    falling = part[-3] + jnp.concatenate([jnp.zeros_like(falling), falling])
    rising, falling = both_ways(rising, falling)
    part.update(parts_of(LATE, pieces))
    rising, falling = both_ways(part[2] + rising, part[-2] + falling)
    rising, falling = part[1] + rising, part[-1] + falling
    rising, falling = both_ways(rising, falling)
    summed = part[0] + rising + falling
    summed = summed + other_half(summed)

    whole = {0: summed}
    wanted = lax.dynamic_slice_in_dim(summed, yh * 2 * tile_rows, 2 * tile_rows, 1)
    rising, falling, wanted = together(summed, summed, wanted)
    whole[-1], whole[1] = together(up(rising), down(falling))
    arrived = swapped(wanted)
    whole[-2], whole[2] = together(up(whole[-1]), down(whole[1]))
    kept = lax.dynamic_slice_in_dim(arrived, core * tile_rows, tile_rows, 1)
    given = lax.dynamic_slice_in_dim(arrived, (1 - core) * tile_rows, tile_rows, 1)
    given = other_core(given)
    zero = jnp.int32(0)
    piece = jnp.zeros((2, half_rows, tile_rows), jnp.float32)
    piece = lax.dynamic_update_slice(piece, kept[None], (core, zero, zero))
    piece = lax.dynamic_update_slice(piece, given[None], (1 - core, zero, zero))
    piece = piece.reshape(piece_rows, tile_rows)
    facing = moved(piece, lambda z, yh, core, col: (z, yh, core, col ^ 4))
    near_y = jnp.concatenate([whole[d] for d in NEAR])
    pair = jnp.concatenate([piece, facing])

    def along_x(array, by):
        return moved(
            array, lambda z, yh, core, col: (z, yh, core, col // 4 * 4 + (col % 4 + by) % 4)
        )

    whole[-3], whole[3] = together(up(whole[-2]), down(whole[2]))
    before, after = along_x(pair, 1), along_x(pair, -1)
    other_near_y = other_core(near_y)
    opposite = along_x(pair, 2)
    rising, falling = together(up(whole[-3][:cut]), down(whole[3][cut:]))
    far_y = jnp.concatenate([whole[d] for d in FAR[:-1]] + [rising, falling])
    other_far_y = other_core(far_y)
    products = columns_product(
        core, [pieces[d] for d in NEAR + FAR], [near_y, other_near_y, far_y, other_far_y]
    )

    x_at, side = col % 4, col // 4
    match = [
        flip * 4 + (x_at + by) % 4 for by in (0, -1, 1, 2) for flip in (side, 1 - side)
    ]
    return updated(
        0.5 / sample_count,
        row_index * tile_rows - col * tile_cols,
        [pair, before, after, opposite],
        samples,
        match,
        products,
        omega,
        diag_entries[:, None],
    )


def solution(mesh):
    split = Mesh(mesh.devices.reshape(SIZES), ALL)

    return jax.shard_map(
        per_device,
        mesh=split,
        in_specs=(P(None, COL), P(ROW, COL), P(ROW), P()),
        out_specs=P(ROW, COL),
        check_vma=False,
    )
```
